32 devices in a mesh: seq: 16 (over z, y, x), tp: 2 (over core).
Axes of the slice: x: 2, y: 2, z: 4, core: 2. Of those that a mesh axis runs over, the one named last changes fastest.
Arguments:
- tokens: bfloat16 [8192, 3072], P('seq', 'tp'), may hold values from -6 to 6
- qkv_weight: bfloat16 [3, 3072, 4096], P(None, 'seq', 'tp'), may hold values from -0.109375 to 0.109375
- log_decay: float32 [32, 8192], P('tp', 'seq'), may hold values from -2 to 0, as said below
- norm_gain: float32 [4096], P('tp'), may hold values from 0.5 to 1.5
Outputs:
- attended: bfloat16 [8192, 4096], P('seq', 'tp')
The draws below stay inside these ranges and needn't reach their ends.
Inputs may be any that keep to these rules, and one draw needn't show every extreme that they name: `log_decay`: every entry is negative.
All inputs are finite; a program needn't handle non-finite values.
Results may differ from the reference program's by a relative error of at most 0.007.
Values may be sent and summed in bfloat16 or wider, within the bound.
No kernel may reach another device: no remote copies, remote signals or barrier semaphores. Data moves between devices by JAX's collectives and lax.ppermute only.
A program may use at most 128 MiB of HBM per device.

```python
import jax
import jax.numpy as jnp
from jax import lax

D = 3072
LOCAL_HEAD_COUNT = 32
DH = 128
CH = 256
TOK_DEV = 512
SEQUENCE_TOKENS = 8192


def draw_log_decay(key, part):
    random_split_keys = jax.random.split(key, 7)
    fast_share = 0.5
    fast_heads = jax.random.uniform(random_split_keys[0], (LOCAL_HEAD_COUNT,)) < fast_share
    fast_rate = 1.0 / jax.random.uniform(random_split_keys[1], (LOCAL_HEAD_COUNT,), minval=30.0, maxval=50.0)
    slow_rate = jax.random.uniform(random_split_keys[2], (LOCAL_HEAD_COUNT,), minval=0.15, maxval=0.4) / SEQUENCE_TOKENS
    baseline_decay_rate = jnp.where(fast_heads, fast_rate, slow_rate)
    nblocks = SEQUENCE_TOKENS // TOK_DEV
    block_decay_factor = jnp.exp(jax.random.uniform(random_split_keys[3], (LOCAL_HEAD_COUNT, nblocks), minval=-0.7, maxval=0.7))
    block_decay_factor = jnp.repeat(block_decay_factor, TOK_DEV, axis=1)
    element_decay_factor = jnp.exp(jax.random.uniform(random_split_keys[4], (LOCAL_HEAD_COUNT, SEQUENCE_TOKENS), minval=-0.5, maxval=0.5))
    spike_locations = jax.random.randint(random_split_keys[5], (LOCAL_HEAD_COUNT, 3), 0, SEQUENCE_TOKENS)
    spike_magnitude = jax.random.uniform(random_split_keys[6], (LOCAL_HEAD_COUNT, 3), minval=0.22, maxval=0.45)
    token_offsets = jnp.arange(SEQUENCE_TOKENS)
    decay_spikes = jnp.sum(jnp.where(token_offsets[None, None, :] == spike_locations[:, :, None], spike_magnitude[:, :, None], 0.0), axis=1)
    return -(baseline_decay_rate[:, None] * block_decay_factor * element_decay_factor + decay_spikes)


def level_of(own_key, shape, shards, smallest, largest):
    factor_of, own = 1.0, jax.random.fold_in(own_key, 6)
    for dim, parts in shards:
        heights = jnp.exp(jax.random.uniform(jax.random.fold_in(own, dim), (parts,), jnp.float32, smallest / len(shards), largest / len(shards)))
        factor_of = factor_of * jnp.repeat(heights, shape[dim] // parts).reshape([-1 if axis == dim else 1 for axis in range(len(shape))])
    return factor_of


def gaussian(stream_key, dims, spread, reach, pieces=(), held_as=jnp.bfloat16):
    result = jax.random.normal(stream_key, dims, jnp.float32) * spread
    if len(pieces) > 0:
        result = level_of(stream_key, dims, pieces, -0.22, 0.18) * result
    return jnp.clip(result, min=-reach, max=reach).astype(held_as)


def setup_inputs(seed: int = 0) -> dict:
    streams_of = jax.random.split(jax.random.key(seed), 5)
    return {
        "tokens": gaussian(streams_of[0], (SEQUENCE_TOKENS, D), 1.0, 6.0, ((0, 16), (1, 2))),
        "qkv_weight": gaussian(streams_of[1], (3, D, LOCAL_HEAD_COUNT * DH), D ** -0.5, 0.109375, ((1, 16), (2, 2))),
        "log_decay": draw_log_decay(jax.random.fold_in(streams_of[4], 71), 0),
        "norm_gain": jnp.clip(1.0 + 0.1 * jax.random.normal(streams_of[3], (LOCAL_HEAD_COUNT * DH,), jnp.float32), 0.5, 1.5),
    }


def reference(tokens, qkv_weight, log_decay, norm_gain):
    proj_query = jnp.dot(tokens, qkv_weight[0], preferred_element_type=jnp.float32)
    proj_key = jnp.dot(tokens, qkv_weight[1], preferred_element_type=jnp.float32)
    proj_value = jnp.dot(tokens, qkv_weight[2], preferred_element_type=jnp.float32)
    queries = (jax.nn.silu(proj_query) * (1.0 / jnp.sqrt(jnp.float32(DH)))).astype(jnp.bfloat16)
    key_rows = jax.nn.silu(proj_key).astype(jnp.bfloat16)
    value_rows = proj_value.astype(jnp.bfloat16)
    nblocks = SEQUENCE_TOKENS // CH

    def split_heads(matrix):
        return matrix.reshape(nblocks, CH, LOCAL_HEAD_COUNT, DH).transpose(0, 2, 1, 3)
    decay_blocks = log_decay.reshape(LOCAL_HEAD_COUNT, nblocks, CH).transpose(1, 0, 2)
    causal = jnp.arange(CH)[:, None] >= jnp.arange(CH)[None, :]

    def advance(state, block_data):
        query_blk, key_blk, value_blk, decay_blk = block_data
        cum_log = jnp.cumsum(decay_blk, axis=-1)
        block_total = cum_log[:, -1]
        cum_gap = cum_log[:, :, None] - cum_log[:, None, :]
        weights = jnp.where(causal[None], jnp.exp(jnp.where(causal[None], cum_gap, 0.0)), 0.0)
        query_f = query_blk.astype(jnp.float32)
        key_f = key_blk.astype(jnp.float32)
        value_f = value_blk.astype(jnp.float32)
        scores = jnp.einsum('htd,hsd->hts', query_f, key_f)
        mixed = (scores * weights).astype(jnp.bfloat16)
        intra = jnp.einsum('hts,hsd->htd', mixed.astype(jnp.float32), value_f)
        inter = jnp.exp(cum_log)[:, :, None] * jnp.einsum('htd,hde->hte', query_f, state, precision=lax.Precision.HIGHEST)
        keyed = (key_f * jnp.exp(block_total[:, None] - cum_log)[:, :, None]).astype(jnp.bfloat16)
        block_state = jnp.einsum('hsd,hse->hde', keyed.astype(jnp.float32), value_f, precision=lax.Precision.HIGHEST)
        new_state = jnp.exp(block_total)[:, None, None] * state + block_state
        return (new_state, intra + inter)
    initial = jnp.zeros((LOCAL_HEAD_COUNT, DH, DH), jnp.float32)
    _, raw = lax.scan(advance, initial, (split_heads(queries), split_heads(key_rows), split_heads(value_rows), decay_blocks))
    raw = raw.transpose(0, 2, 1, 3).reshape(SEQUENCE_TOKENS, LOCAL_HEAD_COUNT, DH)
    mean_square = lax.optimization_barrier(jnp.mean(raw * raw, axis=-1, keepdims=True))
    normed = raw * lax.rsqrt(mean_square + 1e-06) * norm_gain.reshape(LOCAL_HEAD_COUNT, DH)[None]
    return normed.astype(jnp.bfloat16).reshape(SEQUENCE_TOKENS, LOCAL_HEAD_COUNT * DH)
```

```python
import functools

import jax
import jax.numpy as jnp
from jax import lax
from jax.experimental import pallas as pl
from jax.experimental.pallas import tpu as pltpu
from jax.sharding import PartitionSpec as P

DH = 128
CH = 256
X_BIT, Y_BIT, Z_BIT = 0, 1, 2
GROUPS = 4
QUARTER = (0, 1 << Z_BIT, 1 << X_BIT, (1 << Z_BIT) | (1 << X_BIT))
F32 = jnp.float32
BF16 = jnp.bfloat16


def swap_seq(array, mask, count):
    return lax.ppermute(array, "seq", [(s, s ^ mask) for s in range(count)])


def swap_tp(array, mask, count):
    return lax.ppermute(array, "tp", [(s, s ^ mask) for s in range(count)])


def group_of(seq):
    return ((seq >> Z_BIT) & 1) * 2 + ((seq >> X_BIT) & 1)


def relative_block(step, seq):
    z = ((step >> 1) & 1) ^ ((seq >> Z_BIT) & 1)
    x = (step & 1) ^ ((seq >> X_BIT) & 1)
    return x * 2 + z


class Layout:
    def __init__(self, tp, masks, rows, depth, source_rows, width):
        self.tp, self.masks, self.rows, self.depth = tp, masks, rows, depth
        self.source_rows, self.width = source_rows, width
        self.n_tokens = GROUPS * tp
        self.n_weights = len(masks)

    def scratch(self):
        copies = sum(len(m) for m in self.masks)
        return [
            pltpu.VMEM((2, self.tp, self.rows, self.depth), BF16),
            pltpu.VMEM((self.tp * self.depth, self.width), BF16),
            pltpu.SemaphoreType.DMA((2, self.tp)),
            pltpu.SemaphoreType.DMA((copies,)),
        ]


def project(layout, me, tokens, weights, held, matrix, token_sem, weight_sem):
    step = pl.program_id(0)
    seq, core = me[0], me[1]

    def start_tokens(at, slot):
        wanted = relative_block(at, seq)
        for block in range(GROUPS):

            @pl.when(wanted == block)
            def _():
                for part in range(layout.tp):
                    pltpu.make_async_copy(
                        tokens[block * layout.tp + part], held.at[slot, part], token_sem.at[slot, part]
                    ).start()

    def weight_copies():
        number = 0
        for array, masks in zip(weights, layout.masks):
            for place, mask in enumerate(masks):
                row = pl.multiple_of((seq ^ mask) * layout.source_rows, layout.source_rows)
                yield pltpu.make_async_copy(
                    array.at[place], matrix.at[pl.ds(row, layout.source_rows), :], weight_sem.at[number]
                )
                number += 1

    @pl.when(step == 0)
    def _():
        for copy in weight_copies():
            copy.start()
        start_tokens(0, 0)

    @pl.when(step + 1 < pl.num_programs(0))
    def _():
        start_tokens(step + 1, (step + 1) & 1)

    @pl.when(step == 0)
    def _():
        for copy in weight_copies():
            copy.wait()

    slot = step & 1
    total = None
    for part in range(layout.tp):
        pltpu.make_async_copy(tokens[part], held.at[slot, part], token_sem.at[slot, part]).wait()
        row = pl.multiple_of((core ^ part) * layout.depth, layout.depth)
        term = jnp.dot(
            held[slot, part], matrix[pl.ds(row, layout.depth), :], preferred_element_type=F32
        )
        total = term if total is None else total + term
    return total


def next_state(state, keys, values, decay):
    last = decay[CH - 1 : CH, :]
    keyed = (keys.astype(F32) * jnp.exp(last - decay)).astype(BF16)
    outer = lax.dot_general(keyed, values, (((0,), (0,)), ((), ())), preferred_element_type=F32)
    return jnp.exp(last) * state + outer


def kv_kernel(layout, head, me, *refs):
    tokens, refs = refs[: layout.n_tokens], refs[layout.n_tokens :]
    weights, refs = refs[: layout.n_weights], refs[layout.n_weights :]
    decay_ref, kv_ref, state_ref, held, matrix, token_sem, weight_sem = refs
    projected = project(layout, me, tokens, weights, held, matrix, token_sem, weight_sem)
    keys = jax.nn.silu(projected[:, :DH]).astype(BF16)
    values = projected[:, DH:].astype(BF16)
    kv_ref[:, :DH] = keys
    kv_ref[:, DH:] = values

    @pl.when(pl.program_id(0) % 2 == 0)
    def _():
        state_ref[...] = jnp.zeros_like(state_ref)

    state = state_ref[0]
    for block in range(layout.rows // CH):
        at = slice(block * CH, (block + 1) * CH)
        state = next_state(state, keys[at], values[at], decay_ref[at, head : head + 1])
    state_ref[0] = state


def attend_kernel(layout, first, count, me, *refs):
    tokens, refs = refs[: layout.n_tokens], refs[layout.n_tokens :]
    weights, refs = refs[: layout.n_weights], refs[layout.n_weights :]
    kv_refs, refs = refs[:count], refs[count:]
    column_ref, row_ref, enter_ref, gain_ref, out_ref = refs[:5]
    held, matrix, token_sem, weight_sem, state_ref = refs[5:]
    projected = project(layout, me, tokens, weights, held, matrix, token_sem, weight_sem)
    queries = (jax.nn.silu(projected) * (1.0 / jnp.sqrt(F32(DH)))).astype(BF16)

    @pl.when(pl.program_id(0) % 2 == 0)
    def _():
        state_ref[...] = enter_ref[:, 0]

    causal = lax.broadcasted_iota(jnp.int32, (CH, CH), 0) >= lax.broadcasted_iota(
        jnp.int32, (CH, CH), 1
    )
    for index in range(count):
        head = first + index
        lanes = slice(index * DH, (index + 1) * DH)
        state = state_ref[index]
        for block in range(layout.rows // CH):
            at = slice(block * CH, (block + 1) * CH)
            query = queries[at, lanes]
            keys = kv_refs[index][at, :DH]
            values = kv_refs[index][at, DH:]
            decay = column_ref[at, head : head + 1]
            gap = decay - row_ref[head : head + 1, at]
            weight = jnp.where(causal, jnp.exp(jnp.where(causal, gap, 0.0)), 0.0)
            scores = lax.dot_general(
                query, keys, (((1,), (1,)), ((), ())), preferred_element_type=F32
            )
            mixed = (scores * weight).astype(BF16)
            intra = jnp.dot(mixed, values, preferred_element_type=F32)
            high = state.astype(BF16)
            low = (state - high.astype(F32)).astype(BF16)
            inter = jnp.dot(query, high, preferred_element_type=F32) + jnp.dot(
                query, low, preferred_element_type=F32
            )
            raw = intra + jnp.exp(decay) * inter
            mean_square = jnp.mean(raw * raw, axis=-1, keepdims=True)
            normed = raw * lax.rsqrt(mean_square + 1e-06) * gain_ref[:, lanes]
            out_ref[0, at, lanes] = normed.astype(BF16)
            state = next_state(state, keys, values, decay)
        state_ref[index] = state


def place_kernel(places, width, me, *refs):
    out_ref = refs[-1]
    own = group_of(me[0])
    for (group, first, size), piece in zip(places, refs[:-1]):
        column = pl.multiple_of((own ^ group) * width + first, DH)
        out_ref[:, pl.ds(column, size)] = piece[0]


def body(seq_count, tp_count, tokens, qkv_weight, log_decay, norm_gain):
    rows, depth = tokens.shape
    source_rows, width_here = qkv_weight.shape[1:]
    heads = width_here // DH // GROUPS
    unit_heads = min(2, heads)
    group_width = heads * DH
    me_seq = lax.axis_index("seq")
    me = jnp.stack([me_seq, lax.axis_index("tp")]).astype(jnp.int32)
    own = group_of(me_seq)
    swap = functools.partial(swap_seq, count=seq_count)
    high_masks = [1 << bit for bit in range(Z_BIT + 1, seq_count.bit_length() - 1)]
    y_mask, z_mask, x_mask = 1 << Y_BIT, 1 << Z_BIT, 1 << X_BIT

    split = qkv_weight.reshape(3, source_rows, GROUPS, group_width)
    by_group = [
        lax.dynamic_index_in_dim(split, own ^ group, 2, keepdims=False) for group in range(GROUPS)
    ]

    def gather_unit(pick):
        mine, over_x, over_z, over_both = [pick(group) for group in by_group]
        received = swap(jnp.stack([over_z, over_both]), z_mask)
        crossed = swap(jnp.stack([over_x, received[1]]), x_mask)
        held = [(jnp.stack([mine, received[0], crossed[0], crossed[1]]), QUARTER)]
        for mask in high_masks + [y_mask]:
            held = held + [(swap(array, mask), tuple(m ^ mask for m in masks)) for array, masks in held]
        return held

    def pick_kv(head, group):
        lanes = slice(head * DH, (head + 1) * DH)
        return jnp.concatenate([group[1][:, lanes], group[2][:, lanes]], axis=1)

    def pick_query(first, group):
        return group[0][:, first * DH : (first + unit_heads) * DH]

    decay_split = log_decay.reshape(GROUPS, heads, rows)

    def decay_of(group):
        return lax.dynamic_index_in_dim(decay_split, own ^ group, 0, keepdims=False)

    decay_held = jnp.stack(
        [decay_of(0), swap(decay_of(1), x_mask), swap(decay_of(2), z_mask), swap(decay_of(3), x_mask | z_mask)]
    )
    decay_held = decay_held.reshape(2, 2, heads, rows)
    decay_held = jnp.where((me_seq >> X_BIT) & 1 == 1, decay_held[:, ::-1], decay_held)
    decay_held = jnp.where((me_seq >> Z_BIT) & 1 == 1, decay_held[::-1], decay_held)
    decay_rows = decay_held.reshape(GROUPS, heads, rows).transpose(1, 0, 2)
    running = jnp.cumsum(decay_rows.reshape(heads, GROUPS * rows // CH, CH), axis=-1)
    segment_total = jnp.sum(running[:, :, -1].reshape(heads, 2, 2 * rows // CH), axis=-1)
    running_row = running.reshape(heads, GROUPS * rows)
    running_column = running_row.T

    first_weights = gather_unit(functools.partial(pick_kv, 0))
    token_z = swap(tokens, z_mask)
    token_x = swap(tokens, x_mask)
    token_xz = swap(token_z, x_mask)
    token_parts = []
    for array in (tokens, token_z, token_x, token_xz):
        parts = [array]
        mask = 1
        while mask < tp_count:
            parts = parts + [swap_tp(part, mask, tp_count) for part in parts]
            mask *= 2
        token_parts += parts

    any_spec = pl.BlockSpec(memory_space=pl.ANY)
    kvs, states = [], []
    for head in range(heads):
        held = first_weights if head == 0 else gather_unit(functools.partial(pick_kv, head))
        layout = Layout(tp_count, [m for _, m in held], rows, depth, source_rows, 2 * DH)
        kv, state = pl.pallas_call(
            functools.partial(kv_kernel, layout, head),
            name=f"kv_{head}",
            out_shape=(
                jax.ShapeDtypeStruct((GROUPS * rows, 2 * DH), BF16),
                jax.ShapeDtypeStruct((2, DH, DH), F32),
            ),
            grid_spec=pltpu.PrefetchScalarGridSpec(
                num_scalar_prefetch=1,
                grid=(GROUPS,),
                in_specs=[any_spec] * (layout.n_tokens + layout.n_weights)
                + [pl.BlockSpec((rows, heads), lambda i, me: (i, 0))],
                out_specs=[
                    pl.BlockSpec((rows, 2 * DH), lambda i, me: (i, 0)),
                    pl.BlockSpec((1, DH, DH), lambda i, me: (i // 2, 0, 0)),
                ],
                scratch_shapes=layout.scratch(),
            ),
            cost_estimate=pl.CostEstimate(
                flops=2 * GROUPS * rows * depth * tp_count * 2 * DH,
                bytes_accessed=2 * (GROUPS * rows + 2 * DH) * depth * tp_count,
                transcendentals=GROUPS * rows * DH,
            ),
        )(me, *token_parts, *[array for array, _ in held], running_column)
        kvs.append(kv)
        states.append(state)

    def entering(first):
        local = jnp.stack(states[first : first + unit_heads])
        totals = segment_total[first : first + unit_heads]
        other = swap(local, y_mask)
        other_totals = swap(totals, y_mask)
        late = (me_seq >> Y_BIT) & 1 == 1
        early_state, late_state = jnp.where(late, other, local), jnp.where(late, local, other)
        early_total = jnp.where(late, other_totals, totals)
        late_total = jnp.where(late, totals, other_totals)
        order_state = [early_state[:, 0], late_state[:, 0], early_state[:, 1], late_state[:, 1]]
        order_total = [early_total[:, 0], late_total[:, 0], early_total[:, 1], late_total[:, 1]]
        prefix, reach = [jnp.zeros_like(order_state[0])], [jnp.zeros_like(order_total[0])]
        for state, total in zip(order_state, order_total):
            prefix.append(jnp.exp(total)[:, None, None] * prefix[-1] + state)
            reach.append(reach[-1] + total)
        outer, span = prefix[4], reach[4]
        incoming, inner_reach = jnp.zeros_like(prefix[0]), jnp.zeros_like(reach[0])
        for mask in high_masks:
            other_outer, other_span = swap(outer, mask), swap(span, mask)
            upper = (me_seq & mask) != 0
            passed = jnp.exp(inner_reach)[:, None, None] * other_outer
            incoming = incoming + jnp.where(upper, passed, 0.0)
            inner_reach = inner_reach + jnp.where(upper, other_span, 0.0)
            low_outer = jnp.where(upper, other_outer, outer)
            low_span = jnp.where(upper, other_span, span)
            top_outer = jnp.where(upper, outer, other_outer)
            top_span = jnp.where(upper, span, other_span)
            outer = jnp.exp(top_span)[:, None, None] * low_outer + top_outer
            span = low_span + top_span
        result = []
        for run in range(2):
            before = jnp.where(late, prefix[2 * run + 1], prefix[2 * run])
            since = jnp.where(late, reach[2 * run + 1], reach[2 * run])
            result.append(before + jnp.exp(since)[:, None, None] * incoming)
        return jnp.stack(result, axis=1)

    gain = lax.dynamic_index_in_dim(norm_gain.reshape(GROUPS, 1, group_width), own, 0, keepdims=False)
    places, pieces = [], []
    for first in range(0, heads, unit_heads):
        held = gather_unit(functools.partial(pick_query, first))
        layout = Layout(tp_count, [m for _, m in held], rows, depth, source_rows, unit_heads * DH)
        attended = pl.pallas_call(
            functools.partial(attend_kernel, layout, first, unit_heads),
            name=f"attend_{first}",
            out_shape=jax.ShapeDtypeStruct((GROUPS, rows, unit_heads * DH), BF16),
            grid_spec=pltpu.PrefetchScalarGridSpec(
                num_scalar_prefetch=1,
                grid=(GROUPS,),
                in_specs=[any_spec] * (layout.n_tokens + layout.n_weights)
                + [pl.BlockSpec((rows, 2 * DH), lambda i, me: (i, 0))] * unit_heads
                + [
                    pl.BlockSpec((rows, heads), lambda i, me: (i, 0)),
                    pl.BlockSpec((heads, rows), lambda i, me: (0, i)),
                    pl.BlockSpec((unit_heads, 1, DH, DH), lambda i, me: (0, i // 2, 0, 0)),
                    pl.BlockSpec((1, unit_heads * DH), lambda i, me: (0, 0)),
                ],
                out_specs=pl.BlockSpec(
                    (1, rows, unit_heads * DH), lambda i, me: (relative_block(i, me[0]), 0, 0)
                ),
                scratch_shapes=layout.scratch() + [pltpu.VMEM((unit_heads, DH, DH), F32)],
            ),
            cost_estimate=pl.CostEstimate(
                flops=4 * GROUPS * rows * depth * tp_count * unit_heads * DH,
                bytes_accessed=2 * (GROUPS * rows + 2 * DH) * depth * tp_count,
                transcendentals=GROUPS * rows * CH * unit_heads,
            ),
        )(
            me,
            *token_parts,
            *[array for array, _ in held],
            *kvs[first : first + unit_heads],
            running_column,
            running_row,
            entering(first),
            gain[:, first * DH : (first + unit_heads) * DH],
        )
        for block, (mask, group) in enumerate(zip(QUARTER, (0, 2, 1, 3))):
            piece = attended[block : block + 1]
            pieces.append(piece if mask == 0 else swap(piece, mask))
            places.append((group, first * DH, unit_heads * DH))

    steps = 4
    return pl.pallas_call(
        functools.partial(place_kernel, places, group_width),
        name="place",
        out_shape=jax.ShapeDtypeStruct((rows, width_here), BF16),
        grid_spec=pltpu.PrefetchScalarGridSpec(
            num_scalar_prefetch=1,
            grid=(steps,),
            in_specs=[
                pl.BlockSpec((1, rows // steps, size), lambda i, me: (0, i, 0)) for _, _, size in places
            ],
            out_specs=pl.BlockSpec((rows // steps, width_here), lambda i, me: (i, 0)),
        ),
    )(me, *pieces)


def solution(mesh):
    in_specs = (P("seq", "tp"), P(None, "seq", "tp"), P("tp", "seq"), P("tp"))
    return jax.shard_map(
        functools.partial(body, mesh.shape["seq"], mesh.shape["tp"]),
        mesh=mesh,
        in_specs=in_specs,
        out_specs=P("seq", "tp"),
        check_vma=False,
    )
```
